32 devices in a mesh: fsdp: 4 (over x, core), ctx: 2 (over y), seq: 4 (over z).
Axes of the slice: x: 2, y: 2, z: 4, core: 2. Of those that a mesh axis runs over, the one named last changes fastest.
Arguments:
- tokens: bfloat16 [4, 1536, 2048], P('fsdp', ('ctx', 'seq')), may hold values from -20 to 20
- w_query: bfloat16 [2048, 2048], P(('fsdp', 'ctx'), 'seq'), may hold values from -3 to 3
- w_key: bfloat16 [2048, 2048], P(('fsdp', 'ctx'), 'seq'), may hold values from -3 to 3
- w_value: bfloat16 [2048, 2048], P(('fsdp', 'ctx'), 'seq'), may hold values from -0.125 to 0.125
- w_out: bfloat16 [2048, 2048], P('seq', ('fsdp', 'ctx')), may hold values from -0.125 to 0.125
- w_gate: bfloat16 [2048, 8192], P(('fsdp', 'ctx'), 'seq'), may hold values from -0.125 to 0.125
- w_up: bfloat16 [2048, 8192], P(('fsdp', 'ctx'), 'seq'), may hold values from -0.125 to 0.125
- w_down: bfloat16 [8192, 2048], P('seq', ('fsdp', 'ctx')), may hold values from -0.0625 to 0.0625
- query_gain: bfloat16 [2048], P(('fsdp', 'ctx', 'seq')), may hold values from 0 to 2
- key_gain: bfloat16 [2048], P(('fsdp', 'ctx', 'seq')), may hold values from 0 to 2
- attn_gain: bfloat16 [2048], P(('fsdp', 'ctx', 'seq')), may hold values from 0.099609375 to 1.8984375
- mlp_gain: bfloat16 [2048], P(('fsdp', 'ctx', 'seq')), may hold values from 0.099609375 to 1.8984375
- cotangent: bfloat16 [4, 1536, 2048], P('fsdp', ('ctx', 'seq')), may hold values from -6 to 6
Outputs:
- output: bfloat16 [4, 1536, 2048], P('fsdp', ('ctx', 'seq'))
- grad_tokens: float32 [4, 1536, 2048], P('fsdp', ('ctx', 'seq'))
- grad_w_query: float32 [2048, 2048], P(('fsdp', 'ctx'), 'seq')
- grad_w_key: float32 [2048, 2048], P(('fsdp', 'ctx'), 'seq')
- grad_w_value: float32 [2048, 2048], P(('fsdp', 'ctx'), 'seq')
- grad_w_out: float32 [2048, 2048], P('seq', ('fsdp', 'ctx'))
- grad_w_gate: float32 [2048, 8192], P(('fsdp', 'ctx'), 'seq')
- grad_w_up: float32 [2048, 8192], P(('fsdp', 'ctx'), 'seq')
- grad_w_down: float32 [8192, 2048], P('seq', ('fsdp', 'ctx'))
- grad_query_gain: float32 [2048], P(('fsdp', 'ctx', 'seq'))
- grad_key_gain: float32 [2048], P(('fsdp', 'ctx', 'seq'))
- grad_attn_gain: float32 [2048], P(('fsdp', 'ctx', 'seq'))
- grad_mlp_gain: float32 [2048], P(('fsdp', 'ctx', 'seq'))
The draws below stay inside these ranges and needn't reach their ends.
All inputs are finite; a program needn't handle non-finite values.
Results may differ from the reference program's by a relative error of at most 0.03.
The reference program's roundings to bfloat16 on the way count: a program that leaves them out, or rounds other values in their place, can miss the bound.
Values may be sent and summed in bfloat16 or wider, within the bound.
No kernel may reach another device: no remote copies, remote signals or barrier semaphores. Data moves between devices by JAX's collectives and lax.ppermute only.
A program may use at most 256 MiB of HBM per device.

```python
import jax
import jax.numpy as jnp
from jax import lax

D = 2048
H = 16
HS = 128
FF = 8192
BLOCK = 768
BATCH = 4
LEN = 1536


def projection(key, salt):
    return jax.random.truncated_normal(jax.random.fold_in(key, salt), -6.0, 6.0, (D, D), jnp.float32) * D ** (-0.5)


def draw_w_query(key, part):
    values = projection(key, 11)
    return values.astype(jnp.bfloat16)


def draw_w_key(key, part):
    values = projection(key, 12)
    return values.astype(jnp.bfloat16)


def drawn_gain(key, salt):
    return 1.0 + 0.18 * jax.random.truncated_normal(jax.random.fold_in(key, salt), -5.0, 5.0, (D,), jnp.float32)


def draw_query_gain(key, part):
    values = drawn_gain(key, 21)
    return values.astype(jnp.bfloat16)


def draw_key_gain(key, part):
    values = drawn_gain(key, 31)
    return values.astype(jnp.bfloat16)


def draw_tokens(key, part):
    drawn = jax.random.truncated_normal(jax.random.fold_in(key, 41), -6.0, 6.0, (BATCH, LEN, D), jnp.float32)
    values = drawn
    return values.astype(jnp.bfloat16)


def level_of(key, shape, split, least, largest):
    def one(dim, blocks):
        steps = jax.random.uniform(jax.random.fold_in(jax.random.fold_in(key, 6), dim), (blocks,), jnp.float32, least / len(split), largest / len(split))
        return jnp.repeat(jnp.exp(steps), shape[dim] // blocks).reshape((-1,) + (1,) * (len(shape) - dim - 1))

    level = one(*split[0])
    for cut in split[1:]:
        level = level * one(*cut)
    return level


def normal_values(stream_key, shape, scale, reach, split=(), kind=jnp.bfloat16):
    factor_of = level_of(stream_key, shape, split, -0.22, 0.18) if split else 1.0
    drawn = jax.random.normal(stream_key, shape, jnp.float32) * scale * factor_of
    return jnp.minimum(jnp.maximum(drawn, -reach), reach).astype(kind)


def setup_inputs(seed: int = 0) -> dict:
    seeds = jax.random.split(jax.random.key(seed), 14)
    tokens = draw_tokens(jax.random.fold_in(seeds[13], 71), 0)
    w_query = draw_w_query(jax.random.fold_in(seeds[13], 71), 0)
    w_key = draw_w_key(jax.random.fold_in(seeds[13], 71), 0)
    w_value = normal_values(seeds[3], (D, D), D ** -0.5, 0.125, ((0, 8), (1, 4)))
    w_out = normal_values(seeds[4], (D, D), D ** -0.5, 0.125, ((0, 4), (1, 8)))
    w_gate = normal_values(seeds[5], (D, FF), D ** -0.5, 0.125, ((0, 8), (1, 4)))
    w_up = normal_values(seeds[6], (D, FF), D ** -0.5, 0.125, ((0, 8), (1, 4)))
    w_down = normal_values(seeds[7], (FF, D), FF ** -0.5, 0.0625, ((0, 4), (1, 8)))
    query_gain = draw_query_gain(jax.random.fold_in(seeds[13], 71), 0)
    key_gain = draw_key_gain(jax.random.fold_in(seeds[13], 71), 0)
    attn_gain = jnp.clip(1.0 + 0.18 * jax.random.normal(seeds[10], (D,), jnp.float32), 0.099609375, 1.8984375).astype(jnp.bfloat16)
    mlp_gain = jnp.clip(1.0 + 0.18 * jax.random.normal(seeds[11], (D,), jnp.float32), 0.099609375, 1.8984375).astype(jnp.bfloat16)
    cotangent = normal_values(seeds[12], (BATCH, LEN, D), 1.0, 6.0, ((0, 4), (1, 8)))
    return {"tokens": tokens, "w_query": w_query, "w_key": w_key, "w_value": w_value, "w_out": w_out, "w_gate": w_gate, "w_up": w_up, "w_down": w_down, "query_gain": query_gain, "key_gain": key_gain, "attn_gain": attn_gain, "mlp_gain": mlp_gain, "cotangent": cotangent}


EPSILON = 1e-06
THETA_BASE = 500000.0
HIGHEST = lax.Precision.HIGHEST

@jax.custom_vjp
def low(v):
    return lax.optimization_barrier(v.astype(jnp.bfloat16)).astype(jnp.float32)

@jax.custom_vjp
def low_back(v):
    return v

def low_keep(v):
    return (low(v), None)

def low_pass(kept, grad):
    return (grad,)

def back_keep(v):
    return (v, None)

def back_low(kept, grad):
    return (low(grad),)
low.defvjp(low_keep, low_pass)
low_back.defvjp(back_keep, back_low)

def rms_normed(values):
    return values * lax.rsqrt(lax.optimization_barrier(jnp.mean(values * values, axis=-1, keepdims=True)) + EPSILON)

def rotary(values, positions):
    half_size = HS // 2
    frequency = THETA_BASE ** (-jnp.arange(half_size, dtype=jnp.float32) * 2.0 / HS)
    angles = positions.astype(jnp.float32)[:, None] * frequency[None, :]
    cosine = jnp.cos(angles)[:, None, :]
    sine_part = jnp.sin(angles)[:, None, :]
    first_half = values[..., :half_size]
    second_half = values[..., half_size:]
    return jnp.concatenate([first_half * cosine - second_half * sine_part, second_half * cosine + first_half * sine_part], axis=-1)

def attend(queries, keys_in, values_in):
    factor = HS ** (-0.5)
    columns = jnp.arange(LEN, dtype=jnp.int32)

    def one_block(block_id):
        first_row = block_id * BLOCK
        query_rows = lax.dynamic_slice_in_dim(queries, first_row, BLOCK, 0)
        scores = low_back(jnp.einsum('qhd,khd->hqk', query_rows, keys_in, precision=HIGHEST) * factor)
        row_ids = first_row + jnp.arange(BLOCK, dtype=jnp.int32)
        scores = jnp.where(columns[None, None, :] <= row_ids[None, :, None], scores, -1e+30)
        weights = jax.nn.softmax(scores, axis=-1)
        return jnp.einsum('hqk,khd->qhd', low(weights), values_in, precision=HIGHEST)
    blocks = lax.map(jax.checkpoint(one_block), jnp.arange(LEN // BLOCK, dtype=jnp.int32))
    return blocks.reshape(LEN, H, HS)

def layer(sequence, params):
    w_query, w_key, w_value, w_out, w_gate, w_up, w_down, query_gain, key_gain, attn_gain, mlp_gain = params
    positions = jnp.arange(LEN, dtype=jnp.int32)
    query_pre = low_back(jnp.dot(sequence, w_query, precision=HIGHEST))
    key_pre = low_back(jnp.dot(sequence, w_key, precision=HIGHEST))
    value_low = low(low_back(jnp.dot(sequence, w_value, precision=HIGHEST))).reshape(LEN, H, HS)
    query_rot = low(low_back(rotary((rms_normed(query_pre) * query_gain).reshape(LEN, H, HS), positions)))
    key_rot = low(low_back(rotary((rms_normed(key_pre) * key_gain).reshape(LEN, H, HS), positions)))
    attended = low(low_back(attend(query_rot, key_rot, value_low).reshape(LEN, D)))
    attn_proj = low_back(jnp.dot(attended, w_out, precision=HIGHEST))
    hidden = sequence + rms_normed(attn_proj) * attn_gain
    hidden_low = low(hidden)
    gate_pre = low_back(jnp.dot(hidden_low, w_gate, precision=HIGHEST))
    up_pre = low_back(jnp.dot(hidden_low, w_up, precision=HIGHEST))
    mixed_low = low(jax.nn.silu(gate_pre) * up_pre)
    mlp_proj = low_back(jnp.dot(mixed_low, w_down, precision=HIGHEST))
    return hidden + rms_normed(mlp_proj) * mlp_gain

def reference(tokens, w_query, w_key, w_value, w_out, w_gate, w_up, w_down, query_gain, key_gain, attn_gain, mlp_gain, cotangent):
    params = (w_query.astype(jnp.float32), w_key.astype(jnp.float32), w_value.astype(jnp.float32), w_out.astype(jnp.float32), w_gate.astype(jnp.float32), w_up.astype(jnp.float32), w_down.astype(jnp.float32), query_gain.astype(jnp.float32), key_gain.astype(jnp.float32), attn_gain.astype(jnp.float32), mlp_gain.astype(jnp.float32))

    def forward_all(inputs, weights_all):

        def per_sequence(sequence):
            return layer(sequence, weights_all)
        return lax.map(per_sequence, inputs)
    result, pullback = jax.vjp(forward_all, tokens.astype(jnp.float32), params)
    grad_inputs, grad_params = pullback(cotangent.astype(jnp.float32))
    return (result.astype(jnp.bfloat16), grad_inputs, grad_params[0], grad_params[1], grad_params[2], grad_params[3], grad_params[4], grad_params[5], grad_params[6], grad_params[7], grad_params[8], grad_params[9], grad_params[10])
```

```python
import functools

import jax
import jax.numpy as jnp
from jax import lax
from jax.experimental import pallas as pl
from jax.experimental.pallas import tpu as pltpu
from jax.sharding import PartitionSpec as P


D = 2048
HS = 128
WB = 256
EPSILON = 1e-06
THETA_BASE = 500000.0
MASKED = -1e30
SCALE = HS ** (-0.5)
KB = 384
F32 = jnp.float32
BF16 = jnp.bfloat16
ANY = pl.BlockSpec(memory_space=pl.ANY)
VMEM_LIMIT = 60 * 1024 * 1024

SLOTS = ((0, 0), (1, 0), (2, 0), (2, 1), (3, 0), (4, 0), (5, 0), (5, 1))


def plane_perms():
    core = [(i, i ^ 2) for i in range(8)]
    first = [(i, i ^ (4 if not i & 2 else 1)) for i in range(8)]
    second = [(i, i ^ (1 if not i & 2 else 4)) for i in range(8)]
    return core, first, second


PLANE = ("fsdp", "ctx")


def block_ids():
    fsdp = lax.axis_index("fsdp")
    own = fsdp * 2 + lax.axis_index("ctx")
    is0 = (fsdp % 2) == 0
    first = jnp.where(is0, 4, 1)
    second = jnp.where(is0, 1, 4)
    keep = [own, own ^ first, own ^ second, own ^ 5]
    other = own ^ 2
    send = [other, other ^ second, other ^ first, other ^ 5]
    return jnp.stack(keep + send).astype(jnp.int32)


def gather_plane(own):
    core, first, second = plane_perms()
    near = lax.ppermute(own, PLANE, first)
    far = lax.ppermute(jnp.concatenate([own, near], 0), PLANE, second)
    return (
        own,
        near,
        far,
        lax.ppermute(own, PLANE, core),
        lax.ppermute(near, PLANE, core),
        lax.ppermute(far, PLANE, core),
    )


def after(value, *tokens):
    return lax.optimization_barrier((value,) + tokens)[0]


def to_core(partial):
    return lax.ppermute(partial, PLANE, plane_perms()[0])


def to_second(partial):
    return lax.ppermute(partial, PLANE, plane_perms()[2])


def reduce_end(kept, got):
    rest = kept.astype(F32) + got.astype(F32)
    last = lax.ppermute(rest[1].astype(BF16), PLANE, plane_perms()[1])
    return rest[0] + last.astype(F32)


def seq_sum(values):
    count = lax.axis_size("seq")
    step = 1
    while step < count:
        values = values + lax.ppermute(
            values, "seq", [(i, i ^ step) for i in range(count)]
        )
        step *= 2
    return values


def all_sum(values):
    values = seq_sum(values)
    for step in (2, 4, 1):
        values = values + lax.ppermute(values, PLANE, [(i, i ^ step) for i in range(8)])
    return values


def params(**kw):
    return pltpu.CompilerParams(vmem_limit_bytes=VMEM_LIMIT, **kw)


def cost(flops, nbytes, trans=0):
    return pl.CostEstimate(flops=int(flops), bytes_accessed=int(nbytes), transcendentals=int(trans))


def nn(a, b):
    return lax.dot_general(a, b, (((1,), (0,)), ((), ())), preferred_element_type=F32)


def nt(a, b):
    return lax.dot_general(a, b, (((1,), (1,)), ((), ())), preferred_element_type=F32)


def tn(a, b):
    return lax.dot_general(a, b, (((0,), (0,)), ((), ())), preferred_element_type=F32)


def row_stat(values):
    ones = jnp.ones((8, values.shape[1]), F32)
    return lax.dot_general(
        ones, values, (((1,), (1,)), ((), ())), precision=lax.Precision.HIGHEST, preferred_element_type=F32
    )


def as_column(stat_row):
    wide = jnp.broadcast_to(stat_row[0:1, :], (128, stat_row.shape[1]))
    return jnp.transpose(wide)[:, 0:1]


def block_copies(ids_ref, pieces, source, target, sems):
    out = []
    for s, (piece, inner) in enumerate(SLOTS):
        out.append(
            pltpu.make_async_copy(source(pieces[piece], inner), target(ids_ref[s]), sems.at[s])
        )
    return out


def streamed(step, total, fetch):
    now = lax.rem(step, 2)

    @pl.when(step == 0)
    def _():
        for c in fetch(step, now):
            c.start()

    @pl.when(step + 1 < total)
    def _():
        for c in fetch(step + 1, 1 - now):
            c.start()

    for c in fetch(step, now):
        c.wait()
    return now


def row_block(ids):
    return pl.ds(pl.multiple_of(ids * WB, WB), WB)


def qkv_kernel(groups, ids_ref, x_ref, *rest):
    pieces, (out_ref, stat_ref, buf, sems) = rest[:6], rest[6:]
    r, g = pl.program_id(0), pl.program_id(1)
    step = r * groups + g

    def fetch(at, slot):
        which = lax.rem(at, groups)
        return block_copies(
            ids_ref,
            pieces,
            lambda piece, inner: piece.at[inner, which],
            lambda block: buf.at[slot, row_block(block), :],
            sems.at[slot],
        )

    now = streamed(step, pl.num_programs(0) * groups, fetch)
    value = nn(x_ref[...], buf[now])
    out_ref[0] = value
    stat_ref[...] = row_stat(value * value)


def project_qkv(ids, x, pieces):
    rows = x.shape[0]
    groups, width = pieces[0].shape[1], pieces[0].shape[3]
    rt = min(rows, 768)
    grid = (rows // rt, groups)
    return pl.pallas_call(
        functools.partial(qkv_kernel, groups),
        out_shape=(
            jax.ShapeDtypeStruct((groups, rows, width), F32),
            jax.ShapeDtypeStruct((8 * groups, rows), F32),
        ),
        grid_spec=pltpu.PrefetchScalarGridSpec(
            num_scalar_prefetch=1,
            grid=grid,
            in_specs=[pl.BlockSpec((rt, D), lambda r, g, ids: (r, 0))] + [ANY] * 6,
            out_specs=(
                pl.BlockSpec((1, rt, width), lambda r, g, ids: (g, r, 0)),
                pl.BlockSpec((8, rt), lambda r, g, ids: (g, r)),
            ),
            scratch_shapes=[pltpu.VMEM((2, D, width), BF16), pltpu.SemaphoreType.DMA((2, 8))],
        ),
        compiler_params=params(),
        cost_estimate=cost(2 * rows * D * width * groups, rows * D * 2 + groups * width * (D * 2 + rows * 4)),
        name="project_qkv",
    )(ids, x, *pieces)


def rope(values, cosine, sine, direction):
    out = []
    for h in range(values.shape[1] // HS):
        part = values[:, h * HS : (h + 1) * HS]
        out.append(part * cosine + pltpu.roll(part, HS // 2, 1) * (direction * sine))
    return out


def rope_kernel(qkv_ref, stat_ref, gain_ref, cos_ref, sin_ref, q_ref, kv_ref):
    cosine, sine = cos_ref[...], sin_ref[...]
    for i in range(2):
        factor = lax.rsqrt(as_column(stat_ref[8 * i : 8 * i + 8, :]) / D + EPSILON)
        normed = qkv_ref[i] * factor * gain_ref[i : i + 1, :]
        for h, part in enumerate(rope(normed, cosine, sine, 1.0)):
            if i == 0:
                q_ref[:, h * HS : (h + 1) * HS] = part.astype(BF16)
            else:
                kv_ref[0, :, h * HS : (h + 1) * HS] = part.astype(BF16)
    kv_ref[1] = qkv_ref[2].astype(BF16)


def rotate_qkv(qkv, stats, gains, cosine, sine):
    _, rows, width = qkv.shape
    rt = 384
    return pl.pallas_call(
        rope_kernel,
        out_shape=(
            jax.ShapeDtypeStruct((rows, width), BF16),
            jax.ShapeDtypeStruct((2, rows, width), BF16),
        ),
        grid=(rows // rt,),
        in_specs=[
            pl.BlockSpec((3, rt, width), lambda r: (0, r, 0)),
            pl.BlockSpec((16, rt), lambda r: (0, r)),
            pl.BlockSpec((2, width), lambda r: (0, 0)),
            pl.BlockSpec((rt, HS), lambda r: (r, 0)),
            pl.BlockSpec((rt, HS), lambda r: (r, 0)),
        ],
        out_specs=(
            pl.BlockSpec((rt, width), lambda r: (r, 0)),
            pl.BlockSpec((2, rt, width), lambda r: (0, r, 0)),
        ),
        compiler_params=params(),
        cost_estimate=cost(20 * rows * width, rows * width * 18),
        name="rotate_qkv",
    )(qkv, stats, gains, cosine, sine)


def attn_fwd_kernel(qt, ctx_ref, q_ref, kv_ref, kvr_ref, o_ref, lse_ref, s_scr):
    t = pl.program_id(1)
    span = kv_ref.shape[1]
    far = jnp.where(ctx_ref[0] > 0, span // KB, 0)
    near = (t * qt) // KB + 1
    q = q_ref[...]
    base = span // KB

    def far_scores(i, high):
        s = nt(q, kvr_ref[0, pl.ds(i * KB, KB), :]) * SCALE
        s_scr[i] = s
        return jnp.maximum(high, jnp.max(s, axis=1, keepdims=True))

    def near_scores(i, high):
        s = nt(q, kv_ref[0, pl.ds(i * KB, KB), :]) * SCALE
        row = t * qt + lax.broadcasted_iota(jnp.int32, s.shape, 0)
        col = i * KB + lax.broadcasted_iota(jnp.int32, s.shape, 1)
        s = jnp.where(col <= row, s, MASKED)
        s_scr[base + i] = s
        return jnp.maximum(high, jnp.max(s, axis=1, keepdims=True))

    high = jnp.full((qt, 1), MASKED, F32)
    high = lax.fori_loop(0, far, far_scores, high)
    high = lax.fori_loop(0, near, near_scores, high)

    def weigh(i, total):
        e = jnp.exp(s_scr[i] - high)
        s_scr[i] = e
        return total + jnp.sum(e, axis=1, keepdims=True)

    total = lax.fori_loop(0, far, weigh, jnp.zeros((qt, 1), F32))
    total = lax.fori_loop(base, base + near, weigh, total)
    inverse = 1.0 / total

    def far_out(i, acc):
        return acc + nn((s_scr[i] * inverse).astype(BF16), kvr_ref[1, pl.ds(i * KB, KB), :])

    def near_out(i, acc):
        return acc + nn((s_scr[base + i] * inverse).astype(BF16), kv_ref[1, pl.ds(i * KB, KB), :])

    acc = lax.fori_loop(0, far, far_out, jnp.zeros((qt, HS), F32))
    acc = lax.fori_loop(0, near, near_out, acc)
    o_ref[...] = acc.astype(BF16)
    lse_ref[0] = jnp.broadcast_to(high + jnp.log(total), (qt, HS))


def attention_fwd(ctx, q, kv, kv_far, qt):
    rows, width = q.shape
    heads = width // HS
    return pl.pallas_call(
        functools.partial(attn_fwd_kernel, qt),
        out_shape=(
            jax.ShapeDtypeStruct((rows, width), BF16),
            jax.ShapeDtypeStruct((heads, rows, HS), F32),
        ),
        grid_spec=pltpu.PrefetchScalarGridSpec(
            num_scalar_prefetch=1,
            grid=(heads, rows // qt),
            in_specs=[
                pl.BlockSpec((qt, HS), lambda h, t, c: (t, h)),
                pl.BlockSpec((2, rows, HS), lambda h, t, c: (0, 0, h)),
                pl.BlockSpec((2, rows, HS), lambda h, t, c: (0, 0, h)),
            ],
            out_specs=(
                pl.BlockSpec((qt, HS), lambda h, t, c: (t, h)),
                pl.BlockSpec((1, qt, HS), lambda h, t, c: (h, t, 0)),
            ),
            scratch_shapes=[pltpu.VMEM((2 * rows // KB, qt, KB), F32)],
        ),
        compiler_params=params(),
        cost_estimate=cost(6 * rows * rows * width, rows * width * 14, 2 * rows * rows * heads),
        name="attention_fwd",
    )(ctx, q, kv, kv_far)


def attn_bwd_kernel(
    qt, ctx_ref, q_ref, do_ref, kv_ref, kvr_ref, lse_ref, dq_ref, dkv_ref, dkvr_ref, p_scr, dp_scr, near_acc, far_acc
):
    t = pl.program_id(1)
    span = kv_ref.shape[1]
    far = jnp.where(ctx_ref[0] > 0, span // KB, 0)
    near = (t * qt) // KB + 1
    base = span // KB
    q, do = q_ref[...], do_ref[...]
    lse = lse_ref[0][:, 0:1]

    @pl.when(t == 0)
    def _():
        near_acc[...] = jnp.zeros_like(near_acc)
        far_acc[...] = jnp.zeros_like(far_acc)

    def far_first(i, delta):
        at = pl.ds(i * KB, KB)
        p = jnp.exp(nt(q, kvr_ref[0, at, :]) * SCALE - lse)
        dp = nt(do, kvr_ref[1, at, :])
        p_scr[i] = p
        dp_scr[i] = dp
        return delta + jnp.sum(p * dp, axis=1, keepdims=True)

    def near_first(i, delta):
        at = pl.ds(i * KB, KB)
        s = nt(q, kv_ref[0, at, :]) * SCALE
        row = t * qt + lax.broadcasted_iota(jnp.int32, s.shape, 0)
        col = i * KB + lax.broadcasted_iota(jnp.int32, s.shape, 1)
        p = jnp.exp(jnp.where(col <= row, s, MASKED) - lse)
        dp = nt(do, kv_ref[1, at, :])
        p_scr[base + i] = p
        dp_scr[base + i] = dp
        return delta + jnp.sum(p * dp, axis=1, keepdims=True)

    delta = lax.fori_loop(0, far, far_first, jnp.zeros((qt, 1), F32))
    delta = lax.fori_loop(0, near, near_first, delta)

    def second(offset, keys_ref, acc_ref):
        def body(i, dq):
            at = pl.ds(i * KB, KB)
            p = p_scr[offset + i]
            ds = (p * (dp_scr[offset + i] - delta)).astype(BF16)
            acc_ref[0, at, :] += tn(ds, q)
            acc_ref[1, at, :] += tn(p.astype(BF16), do)
            return dq + nn(ds, keys_ref[0, at, :])

        return body

    dq = lax.fori_loop(0, far, second(0, kvr_ref, far_acc), jnp.zeros((qt, HS), F32))
    dq = lax.fori_loop(0, near, second(base, kv_ref, near_acc), dq)
    dq_ref[...] = (dq * SCALE).astype(BF16)

    @pl.when(t == pl.num_programs(1) - 1)
    def _():
        dkv_ref[0] = near_acc[0] * SCALE
        dkv_ref[1] = near_acc[1]
        dkvr_ref[0] = (far_acc[0] * SCALE).astype(BF16)
        dkvr_ref[1] = far_acc[1].astype(BF16)


def attention_bwd(ctx, q, do, kv, kv_far, lse, qt, head0, heads):
    rows = q.shape[0]
    width = heads * HS
    return pl.pallas_call(
        functools.partial(attn_bwd_kernel, qt),
        out_shape=(
            jax.ShapeDtypeStruct((rows, width), BF16),
            jax.ShapeDtypeStruct((2, rows, width), F32),
            jax.ShapeDtypeStruct((2, rows, width), BF16),
        ),
        grid_spec=pltpu.PrefetchScalarGridSpec(
            num_scalar_prefetch=1,
            grid=(heads, rows // qt),
            in_specs=[
                pl.BlockSpec((qt, HS), lambda h, t, c: (t, h + head0)),
                pl.BlockSpec((qt, HS), lambda h, t, c: (t, h + head0)),
                pl.BlockSpec((2, rows, HS), lambda h, t, c: (0, 0, h + head0)),
                pl.BlockSpec((2, rows, HS), lambda h, t, c: (0, 0, h + head0)),
                pl.BlockSpec((1, qt, HS), lambda h, t, c: (h + head0, t, 0)),
            ],
            out_specs=(
                pl.BlockSpec((qt, HS), lambda h, t, c: (t, h)),
                pl.BlockSpec((2, rows, HS), lambda h, t, c: (0, 0, h)),
                pl.BlockSpec((2, rows, HS), lambda h, t, c: (0, 0, h)),
            ),
            scratch_shapes=[
                pltpu.VMEM((2 * rows // KB, qt, KB), F32),
                pltpu.VMEM((2 * rows // KB, qt, KB), F32),
                pltpu.VMEM((2, rows, HS), F32),
                pltpu.VMEM((2, rows, HS), F32),
            ],
        ),
        compiler_params=params(),
        cost_estimate=cost(14 * rows * rows * width, rows * width * 30, 2 * rows * rows * heads),
        name="attention_bwd",
    )(ctx, q, do, kv, kv_far, lse)


def norm_factor(values):
    return lax.rsqrt(jnp.mean(values * values, axis=-1, keepdims=True) + EPSILON)


def norm_back(upstream, normed, factor):
    return factor * (upstream - normed * jnp.mean(upstream * normed, axis=-1, keepdims=True))


def out_kernel(tiles, owned, ids_ref, z_ref, o_ref, x_ref, gain_ref, *rest):
    pieces, (hb_ref, own_ref, o_scr, a_scr, buf, sems) = rest[:6], rest[6:]
    r, j = pl.program_id(0), pl.program_id(1)
    per = 8 // tiles
    steps = pl.num_programs(0) * tiles
    step = r * tiles + j
    now = lax.rem(step, 2)

    def each(at, slot, act):
        which = lax.rem(at, tiles)
        for s, (piece, inner) in enumerate(SLOTS):
            local = ids_ref[s] - which * per

            @pl.when(jnp.logical_and(local >= 0, local < per))
            def _(s=s, piece=piece, inner=inner, local=local):
                act(
                    pltpu.make_async_copy(
                        pieces[piece].at[inner],
                        buf.at[slot, :, pl.ds(pl.multiple_of(local * WB, WB), WB)],
                        sems.at[slot, s],
                    )
                )

    @pl.when(step == 0)
    def _():
        each(step, now, lambda c: c.start())

    @pl.when(step + 1 < steps)
    def _():
        each(step + 1, 1 - now, lambda c: c.start())

    @pl.when(j == 0)
    def _():
        width = o_ref.shape[2]
        for g in range(o_ref.shape[0]):
            o_scr[:, g * width : (g + 1) * width] = o_ref[g]

    each(step, now, lambda c: c.wait())
    tile = per * WB
    a_scr[:, pl.ds(pl.multiple_of(j * tile, tile), tile)] = nn(o_scr[...], buf[now])

    @pl.when(j == tiles - 1)
    def _():
        rt = a_scr.shape[0]
        first = z_ref[0] * owned

        @pl.when(lax.div(first, rt) == r)
        def _():
            own_ref[...] = a_scr[pl.ds(pl.multiple_of(lax.rem(first, rt), owned), owned), :]

        a = a_scr[...]
        hidden = x_ref[...].astype(F32) + a * norm_factor(a) * gain_ref[...]
        hb_ref[...] = hidden.astype(BF16)


def project_out(ids, z, o_all, x, gain, pieces, owned):
    groups, rows, width = o_all.shape
    rt = min(rows, 768)
    tiles = 4
    return pl.pallas_call(
        functools.partial(out_kernel, tiles, owned),
        out_shape=(
            jax.ShapeDtypeStruct((rows, D), BF16),
            jax.ShapeDtypeStruct((owned, D), F32),
        ),
        grid_spec=pltpu.PrefetchScalarGridSpec(
            num_scalar_prefetch=2,
            grid=(rows // rt, tiles),
            in_specs=[
                pl.BlockSpec((groups, rt, width), lambda r, j, i, z: (0, r, 0)),
                pl.BlockSpec((rt, D), lambda r, j, i, z: (r, 0)),
                pl.BlockSpec((1, D), lambda r, j, i, z: (0, 0)),
            ]
            + [ANY] * 6,
            out_specs=(
                pl.BlockSpec((rt, D), lambda r, j, i, z: (r, 0)),
                pl.BlockSpec((owned, D), lambda r, j, i, z: (0, 0)),
            ),
            scratch_shapes=[
                pltpu.VMEM((rt, D), BF16),
                pltpu.VMEM((rt, D), F32),
                pltpu.VMEM((2, D, D // tiles), BF16),
                pltpu.SemaphoreType.DMA((2, 8)),
            ],
        ),
        compiler_params=params(),
        cost_estimate=cost(2 * rows * D * D, rows * D * 6 + D * D * 2),
        name="project_out",
    )(ids, z, o_all, x, gain, *pieces)


def gate_kernel(tiles, ids_ref, hb_ref, *rest):
    pieces, (gu_ref, z_ref, buf, sems) = rest[:6], rest[6:]
    r, j = pl.program_id(0), pl.program_id(1)
    tile = z_ref.shape[1]

    def fetch(at, slot):
        column = pl.ds(pl.multiple_of(lax.rem(at, tiles) * tile, tile), tile)
        out = []
        for g in range(2):
            out += block_copies(
                ids_ref,
                pieces,
                lambda piece, inner: piece.at[inner, g, :, column],
                lambda block: buf.at[slot, row_block(block), g * tile : (g + 1) * tile],
                sems.at[slot, g],
            )
        return out

    now = streamed(r * tiles + j, pl.num_programs(0) * tiles, fetch)
    both = nn(hb_ref[...], buf[now])
    gate, up = both[:, :tile], both[:, tile:]
    gu_ref[0] = gate
    gu_ref[1] = up
    z_ref[...] = (gate * jax.nn.sigmoid(gate) * up).astype(BF16)


def mlp_gate(ids, hb, pieces):
    rows = hb.shape[0]
    hidden = pieces[0].shape[3]
    rt = min(rows, 768)
    tile = min(hidden, 512)
    tiles = hidden // tile
    return pl.pallas_call(
        functools.partial(gate_kernel, tiles),
        out_shape=(
            jax.ShapeDtypeStruct((2, rows, hidden), F32),
            jax.ShapeDtypeStruct((rows, hidden), BF16),
        ),
        grid_spec=pltpu.PrefetchScalarGridSpec(
            num_scalar_prefetch=1,
            grid=(rows // rt, tiles),
            in_specs=[pl.BlockSpec((rt, D), lambda r, j, ids: (r, 0))] + [ANY] * 6,
            out_specs=(
                pl.BlockSpec((2, rt, tile), lambda r, j, ids: (0, r, j)),
                pl.BlockSpec((rt, tile), lambda r, j, ids: (r, j)),
            ),
            scratch_shapes=[pltpu.VMEM((2, D, 2 * tile), BF16), pltpu.SemaphoreType.DMA((2, 2, 8))],
        ),
        compiler_params=params(),
        cost_estimate=cost(4 * rows * D * hidden, rows * D * 2 + hidden * (rows * 10 + D * 4), rows * hidden),
        name="mlp_gate",
    )(ids, hb, *pieces)


def down_kernel(tiles, ids_ref, z_ref, *rest):
    pieces, (m_ref, buf, sems) = rest[:6], rest[6:]
    r, j = pl.program_id(0), pl.program_id(1)
    steps = pl.num_programs(0) * tiles
    step = r * tiles + j
    now = lax.rem(step, 2)
    per = 8 // tiles

    def each(at, slot, act):
        which = lax.rem(at, tiles)
        for s, (piece, inner) in enumerate(SLOTS):
            local = ids_ref[s] - which * per

            @pl.when(jnp.logical_and(local >= 0, local < per))
            def _(s=s, piece=piece, inner=inner, local=local):
                act(
                    pltpu.make_async_copy(
                        pieces[piece].at[inner],
                        buf.at[slot, :, pl.ds(pl.multiple_of(local * WB, WB), WB)],
                        sems.at[slot, s],
                    )
                )

    @pl.when(step == 0)
    def _():
        each(step, now, lambda c: c.start())

    @pl.when(step + 1 < steps)
    def _():
        each(step + 1, 1 - now, lambda c: c.start())

    each(step, now, lambda c: c.wait())
    m_ref[...] = nn(z_ref[...], buf[now]).astype(BF16)


def mlp_down(ids, mixed, pieces):
    rows, hidden = mixed.shape
    rt = min(rows, 768)
    tiles = 4
    tile = D // tiles
    return pl.pallas_call(
        functools.partial(down_kernel, tiles),
        out_shape=jax.ShapeDtypeStruct((rows, D), BF16),
        grid_spec=pltpu.PrefetchScalarGridSpec(
            num_scalar_prefetch=1,
            grid=(rows // rt, tiles),
            in_specs=[pl.BlockSpec((rt, hidden), lambda r, j, ids: (r, 0))] + [ANY] * 6,
            out_specs=pl.BlockSpec((rt, tile), lambda r, j, ids: (r, j)),
            scratch_shapes=[pltpu.VMEM((2, hidden, tile), BF16), pltpu.SemaphoreType.DMA((2, 8))],
        ),
        compiler_params=params(),
        cost_estimate=cost(2 * rows * D * hidden, rows * D * 2 + hidden * (rows * 2 + D * 2)),
        name="mlp_down",
    )(ids, mixed, *pieces)


def turn_kernel(x_ref, a_ref, m_ref, cot_ref, ga_ref, gm_ref, y_ref, dm_ref, gg_ref):
    a, m = a_ref[...], m_ref[...].astype(F32)
    hidden = x_ref[...].astype(F32) + a * norm_factor(a) * ga_ref[...]
    factor = norm_factor(m)
    normed = m * factor
    y_ref[...] = (hidden + normed * gm_ref[...]).astype(BF16)
    dy = cot_ref[...].astype(F32)
    gg_ref[...] = jnp.sum(dy * normed, axis=0, keepdims=True)
    dm_ref[...] = norm_back(dy * gm_ref[...], normed, factor).astype(BF16)


def turn(x, a, m, cotangent, gain_attn, gain_mlp):
    rows = x.shape[0]
    return pl.pallas_call(
        turn_kernel,
        out_shape=(
            jax.ShapeDtypeStruct((rows, D), BF16),
            jax.ShapeDtypeStruct((rows, D), BF16),
            jax.ShapeDtypeStruct((1, D), F32),
        ),
        compiler_params=params(),
        cost_estimate=cost(30 * rows * D, rows * D * 14),
        name="turn",
    )(x, a, m, cotangent, gain_attn, gain_mlp)


def mlp_bwd_kernel(tiles, ids_ref, dm_ref, gu_ref, *rest):
    gu_pieces, down_pieces, (dgu_ref, dh_ref, gu_buf, d_buf, acc, gu_sems, d_sems) = rest[:6], rest[6:12], rest[12:]
    r, j = pl.program_id(0), pl.program_id(1)
    tile = gu_ref.shape[2]

    def fetch(at, slot):
        part = pl.ds(pl.multiple_of(lax.rem(at, tiles) * tile, tile), tile)
        out = block_copies(
            ids_ref,
            down_pieces,
            lambda piece, inner: piece.at[inner, part, :],
            lambda block: d_buf.at[slot, :, row_block(block)],
            d_sems.at[slot],
        )
        for g in range(2):
            out += block_copies(
                ids_ref,
                gu_pieces,
                lambda piece, inner: piece.at[inner, g, :, part],
                lambda block: gu_buf.at[slot, row_block(block), g * tile : (g + 1) * tile],
                gu_sems.at[slot, g],
            )
        return out

    now = streamed(r * tiles + j, pl.num_programs(0) * tiles, fetch)
    dz = nt(dm_ref[...], d_buf[now])
    gate, up = gu_ref[0], gu_ref[1]
    sig = jax.nn.sigmoid(gate)
    dg = (dz * up * sig * (1.0 + gate * (1.0 - sig))).astype(BF16)
    du = (dz * (gate * sig)).astype(BF16)
    dgu_ref[0] = dg
    dgu_ref[1] = du
    part = nt(jnp.concatenate([dg, du], axis=1), gu_buf[now])

    @pl.when(j == 0)
    def _():
        acc[...] = part

    @pl.when(j > 0)
    def _():
        acc[...] += part

    @pl.when(j == tiles - 1)
    def _():
        dh_ref[...] = acc[...].astype(BF16)


def mlp_bwd(ids, dm, gu, gu_pieces, down_pieces):
    rows = dm.shape[0]
    hidden = gu.shape[2]
    rt = min(rows, 768)
    tile = min(hidden, 256)
    tiles = hidden // tile
    return pl.pallas_call(
        functools.partial(mlp_bwd_kernel, tiles),
        out_shape=(
            jax.ShapeDtypeStruct((2, rows, hidden), BF16),
            jax.ShapeDtypeStruct((rows, D), BF16),
        ),
        grid_spec=pltpu.PrefetchScalarGridSpec(
            num_scalar_prefetch=1,
            grid=(rows // rt, tiles),
            in_specs=[
                pl.BlockSpec((rt, D), lambda r, j, ids: (r, 0)),
                pl.BlockSpec((2, rt, tile), lambda r, j, ids: (0, r, j)),
            ]
            + [ANY] * 12,
            out_specs=(
                pl.BlockSpec((2, rt, tile), lambda r, j, ids: (0, r, j)),
                pl.BlockSpec((rt, D), lambda r, j, ids: (r, 0)),
            ),
            scratch_shapes=[
                pltpu.VMEM((2, D, 2 * tile), BF16),
                pltpu.VMEM((2, tile, D), BF16),
                pltpu.VMEM((rt, D), F32),
                pltpu.SemaphoreType.DMA((2, 2, 8)),
                pltpu.SemaphoreType.DMA((2, 8)),
            ],
        ),
        compiler_params=params(),
        cost_estimate=cost(6 * rows * D * hidden, rows * D * 4 + hidden * (rows * 12 + D * 6), rows * hidden),
        name="mlp_bwd",
    )(ids, dm, gu, *gu_pieces, *down_pieces)


def tn_kernel(left_ref, right_ref, *rest):
    value = tn(left_ref[...].reshape(left_ref.shape[-2:]), right_ref[...].reshape(right_ref.shape[-2:]))
    out_ref = rest[-1]
    if len(rest) == 2:
        value = value + rest[0][...].reshape(value.shape).astype(F32)
    out_ref[...] = value.astype(BF16).reshape(out_ref.shape)


def tn_row_blocks(ids, x, grads, first, count, added):
    groups, rows, width = grads.shape
    specs = [
        pl.BlockSpec((rows, WB), lambda g, s, ids: (0, ids[first + s])),
        pl.BlockSpec((1, rows, width), lambda g, s, ids: (g, 0, 0)),
    ]
    args = [x, grads]
    if added is not None:
        specs.append(pl.BlockSpec((1, 1, WB, width), lambda g, s, ids: (first + s, g, 0, 0)))
        args.append(added)
    return pl.pallas_call(
        lambda ids_ref, *refs: tn_kernel(*refs),
        out_shape=jax.ShapeDtypeStruct((count, groups, WB, width), BF16),
        grid_spec=pltpu.PrefetchScalarGridSpec(
            num_scalar_prefetch=1,
            grid=(groups, count),
            in_specs=specs,
            out_specs=pl.BlockSpec((1, 1, WB, width), lambda g, s, ids: (s, g, 0, 0)),
        ),
        compiler_params=params(),
        cost_estimate=cost(2 * count * WB * rows * width * groups, rows * width * groups * 2 + count * groups * WB * width * 4),
        name="tn_row_blocks",
    )(ids, *args)


def tn_col_blocks(ids, left, right, first, count, added):
    rows, width = left.shape
    specs = [
        pl.BlockSpec((rows, width), lambda s, ids: (0, 0)),
        pl.BlockSpec((rows, WB), lambda s, ids: (0, ids[first + s])),
    ]
    args = [left, right]
    if added is not None:
        specs.append(pl.BlockSpec((1, width, WB), lambda s, ids: (first + s, 0, 0)))
        args.append(added)
    return pl.pallas_call(
        lambda ids_ref, *refs: tn_kernel(*refs),
        out_shape=jax.ShapeDtypeStruct((count, width, WB), BF16),
        grid_spec=pltpu.PrefetchScalarGridSpec(
            num_scalar_prefetch=1,
            grid=(count,),
            in_specs=specs,
            out_specs=pl.BlockSpec((1, width, WB), lambda s, ids: (s, 0, 0)),
        ),
        compiler_params=params(),
        cost_estimate=cost(2 * count * WB * rows * width, rows * width * 2 + count * WB * width * 4),
        name="tn_col_blocks",
    )(ids, *args)


def da_kernel(tiles, ids_ref, dhs_ref, cot_ref, a_ref, ga_ref, *rest):
    pieces, (dh_ref, da_ref, gg_ref, do_ref, buf, sems) = rest[:6], rest[6:]
    j = pl.program_id(0)
    tile = do_ref.shape[2]

    def fetch(at, slot):
        part = pl.ds(pl.multiple_of(at * tile, tile), tile)
        return block_copies(
            ids_ref,
            pieces,
            lambda piece, inner: piece.at[inner, part, :],
            lambda block: buf.at[slot, :, row_block(block)],
            sems.at[slot],
        )

    @pl.when(j == 0)
    def _():
        a = a_ref[...]
        factor = norm_factor(a)
        normed = a * factor
        dh = cot_ref[...].astype(F32) + dhs_ref[...].astype(F32)
        dh_ref[...] = dh
        gg_ref[...] = jnp.sum(dh * normed, axis=0, keepdims=True)
        da_ref[...] = norm_back(dh * ga_ref[...], normed, factor).astype(BF16)

    now = streamed(j, tiles, fetch)
    do_ref[0] = nt(da_ref[...], buf[now]).astype(BF16)


def attn_out_back(ids, dh_sum, cotangent, a, gain, pieces, seq_count):
    rows = a.shape[0]
    width = D // seq_count
    full = lambda shape: pl.BlockSpec(shape, lambda j, ids: (0,) * len(shape))
    return pl.pallas_call(
        functools.partial(da_kernel, seq_count),
        out_shape=(
            jax.ShapeDtypeStruct((rows, D), F32),
            jax.ShapeDtypeStruct((rows, D), BF16),
            jax.ShapeDtypeStruct((1, D), F32),
            jax.ShapeDtypeStruct((seq_count, rows, width), BF16),
        ),
        grid_spec=pltpu.PrefetchScalarGridSpec(
            num_scalar_prefetch=1,
            grid=(seq_count,),
            in_specs=[full((rows, D)), full((rows, D)), full((rows, D)), full((1, D))] + [ANY] * 6,
            out_specs=(
                full((rows, D)),
                full((rows, D)),
                full((1, D)),
                pl.BlockSpec((1, rows, width), lambda j, ids: (j, 0, 0)),
            ),
            scratch_shapes=[pltpu.VMEM((2, width, D), BF16), pltpu.SemaphoreType.DMA((2, 8))],
        ),
        compiler_params=params(),
        cost_estimate=cost(2 * rows * D * D, rows * D * 20 + D * D * 2),
        name="attn_out_back",
    )(ids, dh_sum, cotangent, a, gain, *pieces)


def norm_grads(grad, qkv, stat, gain, cosine, sine):
    factor = lax.rsqrt(as_column(stat) / D + EPSILON)
    turned = jnp.concatenate(rope(grad, cosine, sine, -1.0), axis=1)
    return turned, turned * gain, qkv * factor, factor


def key_grads(own, far):
    return (own + far.astype(F32)).astype(BF16)


def joined(parts):
    return parts[0] if len(parts) == 1 else jnp.concatenate(parts, axis=1)


def head_grads(refs, i):
    if i == 0:
        return joined([ref[...] for ref in refs[0::3]])
    return joined([key_grads(own[i - 1], far[i - 1]) for own, far in zip(refs[1::3], refs[2::3])])


def back_stat_kernel(calls, *refs):
    refs, (qkv_ref, stat_ref, gain_ref, cos_ref, sin_ref, sum_ref, gg_ref) = refs[: 3 * calls], refs[3 * calls :]
    cosine, sine = cos_ref[...], sin_ref[...]
    sums = []
    for i in range(2):
        grad = head_grads(refs, i).astype(F32)
        turned, upstream, normed, _ = norm_grads(
            grad, qkv_ref[i], stat_ref[8 * i : 8 * i + 8, :], gain_ref[i : i + 1, :], cosine, sine
        )
        sum_ref[8 * i : 8 * i + 8, :] = row_stat(upstream * normed)
        sums.append(jnp.sum(turned * normed, axis=0, keepdims=True))
    both = jnp.concatenate(sums, axis=0)

    @pl.when(pl.program_id(0) == 0)
    def _():
        gg_ref[...] = both

    @pl.when(pl.program_id(0) > 0)
    def _():
        gg_ref[...] += both


def back_apply_kernel(calls, *refs):
    refs, (qkv_ref, stat_ref, sum_ref, gain_ref, cos_ref, sin_ref, out_ref) = refs[: 3 * calls], refs[3 * calls :]
    cosine, sine = cos_ref[...], sin_ref[...]
    for i in range(2):
        grad = head_grads(refs, i).astype(F32)
        _, upstream, normed, factor = norm_grads(
            grad, qkv_ref[i], stat_ref[8 * i : 8 * i + 8, :], gain_ref[i : i + 1, :], cosine, sine
        )
        mean = as_column(sum_ref[8 * i : 8 * i + 8, :]) / D
        out_ref[i] = (factor * (upstream - normed * mean)).astype(BF16)
    out_ref[2] = head_grads(refs, 2)


def norm_back_specs(calls, rt, width):
    part = width // calls
    return [
        pl.BlockSpec((rt, part), lambda r: (r, 0)),
        pl.BlockSpec((2, rt, part), lambda r: (0, r, 0)),
        pl.BlockSpec((2, rt, part), lambda r: (0, r, 0)),
    ] * calls + [
        pl.BlockSpec((2, rt, width), lambda r: (0, r, 0)),
        pl.BlockSpec((16, rt), lambda r: (0, r)),
    ], [
        pl.BlockSpec((2, width), lambda r: (0, 0)),
        pl.BlockSpec((rt, HS), lambda r: (r, 0)),
        pl.BlockSpec((rt, HS), lambda r: (r, 0)),
    ]


def back_stats(grads, qkv, stats, gains, cosine, sine):
    rows, width = qkv.shape[1:]
    calls = len(grads) // 3
    rt = 384
    head, tail = norm_back_specs(calls, rt, width)
    return pl.pallas_call(
        functools.partial(back_stat_kernel, calls),
        out_shape=(jax.ShapeDtypeStruct((16, rows), F32), jax.ShapeDtypeStruct((2, width), F32)),
        grid=(rows // rt,),
        in_specs=head + tail,
        out_specs=(pl.BlockSpec((16, rt), lambda r: (0, r)), pl.BlockSpec((2, width), lambda r: (0, 0))),
        compiler_params=params(),
        cost_estimate=cost(40 * rows * width, rows * width * 22),
        name="back_stats",
    )(*grads, qkv, stats, gains, cosine, sine)


def back_apply(grads, qkv, stats, sums, gains, cosine, sine):
    rows, width = qkv.shape[1:]
    calls = len(grads) // 3
    rt = 384
    head, tail = norm_back_specs(calls, rt, width)
    return pl.pallas_call(
        functools.partial(back_apply_kernel, calls),
        out_shape=jax.ShapeDtypeStruct((3, rows, width), BF16),
        grid=(rows // rt,),
        in_specs=head + [pl.BlockSpec((16, rt), lambda r: (0, r))] + tail,
        out_specs=pl.BlockSpec((3, rt, width), lambda r: (0, r, 0)),
        compiler_params=params(),
        cost_estimate=cost(40 * rows * width, rows * width * 28),
        name="back_apply",
    )(*grads, qkv, stats, sums, gains, cosine, sine)


def dx_kernel(groups, ids_ref, grad_ref, *rest):
    pieces, (dx_ref, buf, acc, sems) = rest[:6], rest[6:]
    r, g = pl.program_id(0), pl.program_id(1)

    def fetch(at, slot):
        which = lax.rem(at, groups)
        return block_copies(
            ids_ref,
            pieces,
            lambda piece, inner: piece.at[inner, which],
            lambda block: buf.at[slot, row_block(block), :],
            sems.at[slot],
        )

    now = streamed(r * groups + g, pl.num_programs(0) * groups, fetch)
    part = nt(grad_ref[0], buf[now])

    @pl.when(g == 0)
    def _():
        acc[...] = part

    @pl.when(g > 0)
    def _():
        acc[...] += part

    @pl.when(g == groups - 1)
    def _():
        dx_ref[...] = acc[...].astype(BF16)


def input_grads(ids, grads, pieces):
    groups, rows, width = grads.shape
    rt = min(rows, 768)
    return pl.pallas_call(
        functools.partial(dx_kernel, groups),
        out_shape=jax.ShapeDtypeStruct((rows, D), BF16),
        grid_spec=pltpu.PrefetchScalarGridSpec(
            num_scalar_prefetch=1,
            grid=(rows // rt, groups),
            in_specs=[pl.BlockSpec((1, rt, width), lambda r, g, ids: (g, r, 0))] + [ANY] * 6,
            out_specs=pl.BlockSpec((rt, D), lambda r, g, ids: (r, 0)),
            scratch_shapes=[
                pltpu.VMEM((2, D, width), BF16),
                pltpu.VMEM((rt, D), F32),
                pltpu.SemaphoreType.DMA((2, 8)),
            ],
        ),
        compiler_params=params(),
        cost_estimate=cost(2 * groups * rows * D * width, rows * D * 2 + groups * width * (rows * 2 + D * 2)),
        name="input_grads",
    )(ids, grads, *pieces)


def rotary_tables(positions):
    half = HS // 2
    frequency = THETA_BASE ** (-jnp.arange(half, dtype=F32) * 2.0 / HS)
    angles = positions.astype(F32)[:, None] * frequency[None, :]
    cosine, sine = jnp.cos(angles), jnp.sin(angles)
    return jnp.concatenate([cosine, cosine], 1), jnp.concatenate([-sine, sine], 1)


def layer(
    tokens, w_query, w_key, w_value, w_out, w_gate, w_up, w_down, query_gain, key_gain, attn_gain, mlp_gain, cotangent
):
    x_own, cot = tokens[0], cotangent[0]
    owned = x_own.shape[0]
    seq_count = lax.axis_size("seq")
    ctx_index = lax.axis_index("ctx").astype(jnp.int32)
    seq_index = lax.axis_index("seq").astype(jnp.int32)
    width = w_query.shape[1]
    span = owned * seq_count
    ids = block_ids()
    ctx1, seq1 = ctx_index[None], seq_index[None]

    x_all = lax.all_gather(x_own, "seq", axis=0, tiled=True)
    own_gains = jnp.stack([query_gain, key_gain, attn_gain, mlp_gain]).astype(F32)
    gain_at = ids[0] * WB + seq_index * own_gains.shape[1]
    gain_all = all_sum(lax.dynamic_update_slice(jnp.zeros((4, D), F32), own_gains, (0, gain_at)))
    qkv_w = gather_plane(jnp.stack([w_query, w_key, w_value])[None])
    gu_w = gather_plane(after(jnp.stack([w_gate, w_up])[None], qkv_w[1]))
    out_w = gather_plane(after(lax.all_gather(w_out, "seq", axis=0, tiled=True)[None], gu_w[2]))
    down_w = gather_plane(after(w_down[None], out_w[1]))

    qk_gain = lax.dynamic_slice_in_dim(gain_all[:2], seq_index * width, width, 1)
    ga, gm = gain_all[2:3], gain_all[3:4]
    cosine, sine = rotary_tables(ctx_index * span + jnp.arange(span, dtype=jnp.int32))

    qkv, stats = project_qkv(ids, x_all, qkv_w)
    stats = seq_sum(stats[:16])
    q, kv = rotate_qkv(qkv, stats, qk_gain, cosine, sine)
    kv_far = lax.ppermute(kv, "ctx", [(0, 1)])
    o, lse = attention_fwd(ctx1, q, kv, kv_far, owned)

    o_all = lax.all_gather(o, "seq", axis=0)
    hb, a_own = project_out(ids, seq1, o_all, x_all, ga, out_w, owned)
    gu, mixed = mlp_gate(ids, hb, gu_w)
    m_own = lax.psum_scatter(mlp_down(ids, mixed, down_w), "seq", scatter_dimension=0, tiled=True)
    output, dm_own, grad_gm = turn(x_own, a_own, m_own, cot, ga, gm)

    dm = lax.all_gather(dm_own, "seq", axis=0, tiled=True)
    dgu, dh_part = mlp_bwd(ids, dm, gu, gu_w, down_w)
    dh_sum = lax.psum_scatter(dh_part, "seq", scatter_dimension=0, tiled=True)
    gu_sent = tn_row_blocks(ids, hb, dgu, 4, 4, None)
    gu_got = to_core(gu_sent)
    down_sent = tn_col_blocks(ids, after(mixed, gu_sent), dm, 4, 4, None)
    down_got = to_core(down_sent)
    gu_far = tn_row_blocks(ids, after(hb, down_sent), dgu, 2, 2, gu_got)
    gu_got = to_second(gu_far), gu_got
    gu_kept = tn_row_blocks(ids, after(hb, gu_far), dgu, 0, 2, gu_got[1])
    down_far = tn_col_blocks(ids, after(mixed, gu_kept), dm, 2, 2, down_got)
    down_got = to_second(down_far), down_got
    down_kept = tn_col_blocks(ids, after(mixed, down_far), dm, 0, 2, down_got[1])
    dh_sum = after(dh_sum, down_kept)
    dh_own, da_own, grad_ga, do_rows = attn_out_back(ids, dh_sum, cot, a_own, ga, out_w, seq_count)

    do = lax.all_to_all(do_rows, "seq", split_axis=0, concat_axis=0, tiled=True).reshape(span, width)
    da = lax.all_gather(after(da_own, do), "seq", axis=0, tiled=True)
    heads = width // HS
    calls = 2 if heads % 2 == 0 else 1
    grads = []
    for i in range(calls):
        dq, dkv, far = attention_bwd(ctx1, q, do, kv, kv_far, lse, owned, i * heads // calls, heads // calls)
        grads += [dq, dkv, lax.ppermute(far, "ctx", [(1, 0)])]
    sums, grad_qk = back_stats(grads, qkv, stats, qk_gain, cosine, sine)
    sums = seq_sum(sums)
    dqkv = back_apply(grads, qkv, stats, sums, qk_gain, cosine, sine)
    dx_part = input_grads(ids, dqkv, qkv_w)
    dx = lax.psum_scatter(dx_part, "seq", scatter_dimension=0, tiled=True)
    x_late = after(x_all, dx_part)
    qkv_sent = tn_row_blocks(ids, x_late, dqkv, 4, 4, None)
    qkv_got = to_core(qkv_sent)
    o_late = after(o, qkv_sent)
    out_sent = tn_col_blocks(ids, o_late, da, 4, 4, None)
    out_got = to_core(out_sent)
    qkv_far = tn_row_blocks(ids, after(x_late, out_sent), dqkv, 2, 2, qkv_got)
    qkv_got = to_second(qkv_far), qkv_got
    qkv_kept = tn_row_blocks(ids, after(x_late, qkv_far), dqkv, 0, 2, qkv_got[1])
    out_far = tn_col_blocks(ids, after(o_late, qkv_kept), da, 2, 2, out_got)
    out_got = to_second(out_far), out_got
    out_kept = tn_col_blocks(ids, after(o_late, out_far), da, 0, 2, out_got[1])
    grad_gu = reduce_end(gu_kept, gu_got[0])
    grad_down = reduce_end(down_kept, down_got[0])
    grad_qkv = reduce_end(qkv_kept, qkv_got[0])
    grad_out = reduce_end(out_kept, out_got[0])
    grad_tokens = dh_own + dx.astype(F32)

    gain_grads = jnp.concatenate(
        [
            lax.dynamic_update_slice(jnp.zeros((2, D), F32), grad_qk, (0, seq_index * width)),
            grad_ga,
            grad_gm,
        ],
        0,
    )
    gain_own = lax.dynamic_slice(all_sum(gain_grads), (0, gain_at), own_gains.shape)
    return (
        output[None],
        grad_tokens[None],
        grad_qkv[0],
        grad_qkv[1],
        grad_qkv[2],
        grad_out,
        grad_gu[0],
        grad_gu[1],
        grad_down,
        gain_own[0],
        gain_own[1],
        gain_own[2],
        gain_own[3],
    )


def solution(mesh):
    if mesh.shape["fsdp"] != 4 or mesh.shape["ctx"] != 2:
        raise ValueError("unsupported mesh")
    rows, cols = P(("fsdp", "ctx"), "seq"), P("seq", ("fsdp", "ctx"))
    gain = P(("fsdp", "ctx", "seq"))
    data = P("fsdp", ("ctx", "seq"), None)
    return jax.shard_map(
        layer,
        mesh=mesh,
        in_specs=(data, rows, rows, rows, cols, rows, rows, cols, gain, gain, gain, gain, data),
        out_specs=(data, data, rows, rows, rows, cols, rows, rows, cols, gain, gain, gain, gain),
        check_vma=False,
    )
```
